512 devices in a mesh: seq: 64 (over z, x), ch: 8 (over y, core).
Axes of the slice: x: 4, y: 4, z: 16, core: 2. Of those that a mesh axis runs over, the one named last changes fastest.
Arguments:
- signal: float32 [16384, 4096], P('seq', 'ch'), may hold values from -6 to 6
- filters: float32 [16384, 256], P(('seq', 'ch')), may hold values from -1 to 1
- skip_gain: float32 [4096], P('ch'), may hold values from -1 to 1
Outputs:
- filtered: float32 [16384, 4096], P('seq', 'ch')
The draws below stay inside these ranges and needn't reach their ends.
All inputs are finite; a program needn't handle non-finite values.
Results may differ from the reference program's by a relative error of at most 0.00009.
Values sent between devices are 32-bit elements; how exact they have to be, the bound alone decides.
A program may use at most 64 MiB of HBM per device.

```python
import jax
import jax.numpy as jnp
from jax import lax

C = 4096
GROUP = 16
GROUPS = 256
SEQ_LEN = 16384


def draw_filters(key, part):
    keys = jax.random.split(jax.random.fold_in(key, 7), 7)
    length = SEQ_LEN
    slow = jnp.exp(jax.random.uniform(keys[1], (GROUPS,), jnp.float32, jnp.log(0.25 / length), jnp.log(2.0 / length)))
    quick = jnp.exp(jax.random.uniform(keys[2], (GROUPS,), jnp.float32, jnp.log(2.0 / length), jnp.log(1.0 / 30.0)))
    coin = jax.random.bernoulli(keys[0], 0.5, (GROUPS,))
    rates = jnp.where(coin, slow, quick)
    noise = jnp.clip(jax.random.normal(keys[5], (length, GROUPS), jnp.float32), -4.0, 4.0)
    tail_rates = jnp.exp(jax.random.uniform(keys[6], (GROUPS,), jnp.float32, jnp.log(0.25 / length), jnp.log(2.0 / length)))
    digit_places = jax.random.randint(keys[3], (3, GROUPS), 0, length)
    scale_factors = jax.random.uniform(keys[4], (3, GROUPS), jnp.float32, 0.5, 0.8)
    delay_steps = jnp.arange(length, dtype=jnp.int32)[:, None]
    lag_values = delay_steps.astype(jnp.float32)
    scale = jnp.sqrt((1.0 - jnp.exp(-2.0 * rates)) / (1.0 - jnp.exp(-2.0 * rates * length)))
    tail_scale = jnp.sqrt((1.0 - jnp.exp(-2.0 * tail_rates)) / (1.0 - jnp.exp(-2.0 * tail_rates * length)))
    head_profile = jnp.exp(-lag_values * rates[None, :]) * scale[None, :]
    tail_profile = jnp.exp(-lag_values * tail_rates[None, :]) * tail_scale[None, :]
    decay_profile = jnp.sqrt(0.9) * head_profile + jnp.sqrt(0.1) * tail_profile
    for impulse_spike in range(3):
        decay_profile = decay_profile * jnp.where(delay_steps >= digit_places[impulse_spike][None, :], scale_factors[impulse_spike][None, :], 1.0)
    return (noise * decay_profile).astype(jnp.float32)


def level_of(key, dims, shards, smallest, top_value):
    def one(position, shards_of):
        heights = jax.random.uniform(jax.random.fold_in(jax.random.fold_in(key, 6), position), (shards_of,), jnp.float32, smallest / len(shards), top_value / len(shards))
        return jnp.repeat(jnp.exp(heights), dims[position] // shards_of).reshape((-1,) + (1,) * (len(dims) - position - 1))

    gain = one(*shards[0])
    for cut in shards[1:]:
        gain = gain * one(*cut)
    return gain


def scatter_about(stream_key, shape, width, limit, cuts=(), kind=jnp.bfloat16):
    entries = jax.random.normal(stream_key, shape, jnp.float32) * width
    if len(cuts) > 0:
        entries = level_of(stream_key, shape, cuts, -0.22, 0.18) * entries
    return jnp.clip(entries, min=-limit, max=limit).astype(kind)


def setup_inputs(seed: int = 0) -> dict:
    key_list = jax.random.split(jax.random.key(seed), 4)
    return {
        "signal": scatter_about(key_list[0], (SEQ_LEN, C), 1.0, 6.0, ((0, 64), (1, 8)), jnp.float32),
        "filters": draw_filters(jax.random.fold_in(key_list[3], 71), 0),
        "skip_gain": jnp.clip(jax.random.uniform(key_list[2], (C,), jnp.float32, -1.0, 1.0) * level_of(key_list[2], (C,), ((0, 8),), -0.4, 0.0), -1.0, 1.0),
    }


def reference(signal, filters, skip_gain):
    length = signal.shape[0]
    groups = filters.shape[1]
    grouped = jnp.transpose(signal.reshape(length, groups, GROUP), (1, 0, 2))
    kernels = jnp.transpose(filters, (1, 0))

    def convolve(pair):
        block, kernel = pair
        spectrum = jnp.fft.rfft(block, n=2 * length, axis=0)
        response = jnp.fft.rfft(kernel, n=2 * length)
        return jnp.fft.irfft(spectrum * response[:, None], n=2 * length, axis=0)[:length]

    conv = lax.map(convolve, (grouped, kernels))
    conv = jnp.transpose(conv, (1, 0, 2)).reshape(length, groups * GROUP)
    return (conv + skip_gain[None, :] * signal).astype(signal.dtype)
```

```python
import functools

import jax
import jax.numpy as jnp
from jax import lax
from jax.experimental import pallas as pl
from jax.experimental.pallas import tpu as pltpu
from jax.sharding import PartitionSpec as P

GROUP = 16
LANES = 128
MESH = pl.DeviceIdType.MESH
BF = jnp.bfloat16
F32 = jnp.float32


def split(value):
    high = value.astype(BF)
    return high, (value - high.astype(F32)).astype(BF)


def exchange_kernel(
    n, sig_ref, tap_ref, out_ref, xbuf, hbuf, ybuf, xx_hi, xx_lo, strip_hi, strip_lo,
    tap_out, sig_out, out_out, tap_sem, sig_sem, out_sem,
):
    me = lax.axis_index("seq")
    cpd, rows = sig_ref.shape[1], sig_ref.shape[2]
    per = rows // LANES
    barrier = pltpu.get_barrier_semaphore()

    def peer(step):
        return lax.rem(me + step, n)

    @pl.loop(1, n)
    def _(step):
        pl.semaphore_signal(barrier, inc=1, device_id={"seq": peer(step)}, device_id_type=MESH)

    pl.semaphore_wait(barrier, n - 1)

    def tap_copy(step):
        other = peer(step)
        return pltpu.make_async_remote_copy(
            src_ref=tap_ref.at[other // 2], dst_ref=hbuf.at[me + 1], send_sem=tap_out,
            recv_sem=tap_sem, device_id={"seq": other}, device_id_type=MESH,
        )

    def sig_copy(step):
        other = peer(step)
        return pltpu.make_async_remote_copy(
            src_ref=sig_ref.at[other], dst_ref=xbuf.at[me], send_sem=sig_out,
            recv_sem=sig_sem, device_id={"seq": other}, device_id_type=MESH,
        )

    def out_copy(step):
        other = peer(step)
        return pltpu.make_async_remote_copy(
            src_ref=ybuf.at[other], dst_ref=out_ref.at[me], send_sem=out_out,
            recv_sem=out_sem, device_id={"seq": other}, device_id_type=MESH,
        )

    @pl.loop(1, n)
    def _(step):
        tap_copy(step).start()

    @pl.loop(1, n)
    def _(step):
        sig_copy(step).start()

    hbuf[0] = jnp.zeros((1, rows), F32)
    hbuf[me + 1] = tap_ref[me // 2]
    xbuf[me] = sig_ref[me]

    def wait_all(ref, sem):
        whole = ref.at[pl.ds(0, n - 1)]
        pltpu.make_async_copy(whole, whole, sem).wait()

    wait_all(hbuf, tap_sem)

    strip_hi[0] = jnp.zeros((LANES, LANES), BF)
    strip_lo[0] = jnp.zeros((LANES, LANES), BF)

    def build(pair, block):
        spread = jnp.broadcast_to(pair, (LANES, 2 * LANES))
        rolled = pltpu.roll(spread, 0, 1, stride=1, stride_axis=0)[:, LANES:]
        high, low = split(rolled)
        strip_hi[block] = high
        strip_lo[block] = low

    @pl.loop(0, n)
    def _(source):
        before = hbuf[source, :, rows - LANES:]
        build(jnp.concatenate([before, hbuf[source + 1, :, :LANES]], axis=1), source * per + 1)
        for part in range(1, per):
            pair = hbuf[source + 1, :, (part - 1) * LANES:(part + 1) * LANES]
            build(pair, source * per + part + 1)

    wait_all(xbuf, sig_sem)

    total = n * cpd
    pad = xx_hi.shape[0] - total
    high, low = split(xbuf[...].reshape(total, rows))
    zero = jnp.zeros((pad, 2 * rows), BF)
    for where, value in ((xx_hi, high), (xx_lo, low)):
        where[:pad] = zero
        where[pad:, :rows] = value
        where[pad:, rows:] = jnp.concatenate([jnp.zeros((cpd, rows), BF), value[:-cpd]], axis=0)

    def toeplitz(strip, step):
        first = step * 2 * per

        def line(start):
            return jnp.concatenate([strip[start + part] for part in range(per)], axis=1)

        lines = []
        for lag in range(2):
            for part in range(per):
                lines.append(line(first + lag * per + 1 - part))
        return jnp.concatenate(lines, axis=0)

    inner = pad // (2 * cpd) + 1
    buckets = n // (2 * inner)
    for bucket in range(buckets):
        base = bucket * inner * 2 * cpd
        height = total - base
        owner = pl.ds(base // cpd, height // cpd)

        def product(offset, bucket=bucket, height=height):
            step = bucket * inner + offset
            window = pl.ds(pl.multiple_of(pad - 2 * cpd * offset, 2 * cpd), height)
            weight_hi, weight_lo = toeplitz(strip_hi, step), toeplitz(strip_lo, step)
            lhs_hi, lhs_lo = xx_hi[window, :], xx_lo[window, :]
            dot = functools.partial(jnp.dot, preferred_element_type=F32)
            value = dot(lhs_hi, weight_hi) + dot(lhs_lo, weight_hi) + dot(lhs_hi, weight_lo)
            return value.reshape(height // cpd, cpd, rows)

        if bucket == 0:
            ybuf[...] = product(0)
            first = 1
        else:
            first = 0

        @pl.loop(first, inner)
        def _(offset, owner=owner, product=product):
            ybuf[owner] += product(offset)

    @pl.loop(1, n)
    def _(step):
        out_copy(step).start()

    out_ref[me] = ybuf[me]

    wait_all(out_ref, out_sem)
    wait_all(hbuf, tap_out)
    wait_all(xbuf, sig_out)
    wait_all(ybuf, out_out)


def exchange(sig, taps):
    n, cpd, rows = sig.shape
    total, pad = n * cpd, 6 * cpd
    blocks = n * rows // LANES + 1
    vmem = pl.BlockSpec(memory_space=pltpu.VMEM)
    return pl.pallas_call(
        functools.partial(exchange_kernel, n),
        out_shape=jax.ShapeDtypeStruct(sig.shape, F32),
        in_specs=[vmem, vmem],
        out_specs=vmem,
        scratch_shapes=[
            pltpu.VMEM(sig.shape, F32),
            pltpu.VMEM((n + 1, 1, rows), F32),
            pltpu.VMEM(sig.shape, F32),
            pltpu.VMEM((pad + total, 2 * rows), BF),
            pltpu.VMEM((pad + total, 2 * rows), BF),
            pltpu.VMEM((blocks, LANES, LANES), BF),
            pltpu.VMEM((blocks, LANES, LANES), BF),
            *[pltpu.SemaphoreType.DMA] * 6,
        ],
        compiler_params=pltpu.CompilerParams(
            collective_id=0, has_side_effects=True, vmem_limit_bytes=48 * 1024 * 1024
        ),
    )(sig, taps)


def body(signal, filters, skip_gain):
    n = lax.axis_size("seq")
    rows, width = signal.shape
    taps = lax.all_to_all(filters, "ch", split_axis=1, concat_axis=0, tiled=True)
    groups = taps.shape[1]
    taps = taps.T.reshape(groups, 1, rows)
    sig = signal.T.reshape(n, width // n, rows)
    values = exchange(sig, taps)
    return values.reshape(width, rows).T + skip_gain[None, :] * signal


def solution(mesh):
    placed = (P("seq", "ch"), P(("seq", "ch"), None), P("ch"))
    return jax.shard_map(
        body, mesh=mesh, in_specs=placed, out_specs=P("seq", "ch"), check_vma=False
    )
```

```python
import functools

import jax
import jax.numpy as jnp
from jax import lax
from jax.experimental import pallas as pl
from jax.experimental.pallas import tpu as pltpu
from jax.sharding import PartitionSpec as P

GROUP = 16
LANES = 128
MESH = pl.DeviceIdType.MESH
BF = jnp.bfloat16
F32 = jnp.float32


def split(value):
    high = value.astype(BF)
    return high, (value - high.astype(F32)).astype(BF)


def exchange_kernel(
    n, m, sig_in, tap_in, out_ref, sig_ref, part_out, part_in, tap_ref, xbuf, hbuf, ybuf, xx_hi, xx_lo,
    strip_hi, strip_lo, part_send, tap_out, sig_out, out_out, part_sem, tap_sem, sig_sem, out_sem,
):
    me = lax.axis_index("seq")
    mine = lax.axis_index("ch")
    cpd, rows = sig_ref.shape[1], sig_ref.shape[2]
    per = rows // LANES
    barrier = pltpu.get_barrier_semaphore()

    def peer(step):
        away = n // 2 - step // 2
        return lax.rem(me + jnp.where(step % 2 == 1, away, n - away), n)

    @pl.loop(1, n)
    def _(step):
        pl.semaphore_signal(barrier, inc=1, device_id={"seq": peer(step)}, device_id_type=MESH)

    @pl.loop(1, m)
    def _(step):
        pl.semaphore_signal(barrier, inc=1, device_id={"ch": lax.rem(mine + step, m)}, device_id_type=MESH)

    lags = tap_in.shape[0]
    slots = LANES // lags
    tiled = jnp.concatenate([tap_in[...]] * slots, axis=0).T
    lane = lax.broadcasted_iota(jnp.int32, tiled.shape, 1)
    start = lags * lax.rem(mine, slots)
    tiled = jnp.where((lane >= start) & (lane < start + lags), tiled, 0.0)
    part_out[...] = tiled.reshape(part_out.shape)

    for first in range(0, n * cpd, LANES):
        turned = sig_in[:, first:first + LANES].T
        sig_ref[first // cpd:(first + LANES) // cpd] = turned.reshape(LANES // cpd, cpd, rows)

    pl.semaphore_wait(barrier, n + m - 2)

    def part_copy(step):
        other = lax.rem(mine + step, m)
        return pltpu.make_async_remote_copy(
            src_ref=part_out.at[other], dst_ref=part_in.at[mine], send_sem=part_send,
            recv_sem=part_sem, device_id={"ch": other}, device_id_type=MESH,
        )

    def tap_copy(step):
        other = peer(step)
        return pltpu.make_async_remote_copy(
            src_ref=tap_ref.at[other // 2], dst_ref=hbuf.at[me + 1], send_sem=tap_out,
            recv_sem=tap_sem, device_id={"seq": other}, device_id_type=MESH,
        )

    def sig_copy(step):
        other = peer(step)
        return pltpu.make_async_remote_copy(
            src_ref=sig_ref.at[other], dst_ref=xbuf.at[me], send_sem=sig_out,
            recv_sem=sig_sem, device_id={"seq": other}, device_id_type=MESH,
        )

    def out_copy(step):
        other = step
        return pltpu.make_async_remote_copy(
            src_ref=ybuf.at[other], dst_ref=out_ref.at[me], send_sem=out_out,
            recv_sem=out_sem, device_id={"seq": other}, device_id_type=MESH,
        )

    @pl.loop(1, m)
    def _(step):
        part_copy(step).start()

    ahead = n // 4

    @pl.loop(1, ahead)
    def _(step):
        sig_copy(step).start()

    part_in[mine] = part_out[mine]
    whole = part_in.at[pl.ds(0, m - 1)]
    pltpu.make_async_copy(whole, whole, part_sem).wait()
    for half in range(m // slots):
        value = part_in[half * slots]
        for slot in range(1, slots):
            value = value + part_in[half * slots + slot]
        for group in range(n // 2):
            tap_ref[group, :, half * LANES:(half + 1) * LANES] = value[group:group + 1]

    @pl.loop(ahead, ahead + 4)
    def _(step):
        sig_copy(step).start()

    @pl.loop(1, n)
    def _(step):
        tap_copy(step).start()

    @pl.loop(ahead + 4, n)
    def _(step):
        sig_copy(step).start()

    hbuf[0] = jnp.zeros((1, rows), F32)
    hbuf[me + 1] = tap_ref[me // 2]
    xbuf[me] = sig_ref[me]

    def wait_all(ref, sem):
        whole = ref.at[pl.ds(0, n - 1)]
        pltpu.make_async_copy(whole, whole, sem).wait()

    wait_all(hbuf, tap_sem)

    strip_hi[0] = jnp.zeros((LANES, LANES), BF)
    strip_lo[0] = jnp.zeros((LANES, LANES), BF)

    def build(pair, block):
        spread = jnp.broadcast_to(pair, (LANES, 2 * LANES))
        rolled = pltpu.roll(spread, 0, 1, stride=1, stride_axis=0)[:, LANES:]
        high, low = split(rolled)
        strip_hi[block] = high
        strip_lo[block] = low

    @pl.loop(0, n)
    def _(source):
        before = hbuf[source, :, rows - LANES:]
        build(jnp.concatenate([before, hbuf[source + 1, :, :LANES]], axis=1), source * per + 1)
        for part in range(1, per):
            pair = hbuf[source + 1, :, (part - 1) * LANES:(part + 1) * LANES]
            build(pair, source * per + part + 1)

    wait_all(xbuf, sig_sem)

    total = n * cpd
    pad = xx_hi.shape[0] - total
    high, low = split(xbuf[...].reshape(total, rows))
    zero = jnp.zeros((pad, 2 * rows), BF)
    for where, value in ((xx_hi, high), (xx_lo, low)):
        where[:pad] = zero
        where[pad:, :rows] = value
        where[pad:, rows:] = jnp.concatenate([jnp.zeros((cpd, rows), BF), value[:-cpd]], axis=0)

    def toeplitz(strip, step):
        first = step * 2 * per

        def line(start):
            return jnp.concatenate([strip[start + part] for part in range(per)], axis=1)

        lines = []
        for lag in range(2):
            for part in range(per):
                lines.append(line(first + lag * per + 1 - part))
        return jnp.concatenate(lines, axis=0)

    inner = pad // (2 * cpd) + 1
    buckets = n // (2 * inner)
    for bucket in range(buckets):
        base = bucket * inner * 2 * cpd
        height = total - base
        owner = pl.ds(base // cpd, height // cpd)

        def product(offset, bucket=bucket, height=height):
            step = bucket * inner + offset
            window = pl.ds(pl.multiple_of(pad - 2 * cpd * offset, 2 * cpd), height)
            weight_hi, weight_lo = toeplitz(strip_hi, step), toeplitz(strip_lo, step)
            lhs_hi, lhs_lo = xx_hi[window, :], xx_lo[window, :]
            dot = functools.partial(jnp.dot, preferred_element_type=F32)
            value = dot(lhs_hi, weight_hi) + dot(lhs_lo, weight_hi) + dot(lhs_hi, weight_lo)
            return value.reshape(height // cpd, cpd, rows)

        if bucket == 0:
            ybuf[...] = product(0)
            first = 1
        else:
            first = 0

        @pl.loop(first, inner)
        def _(offset, owner=owner, product=product):
            ybuf[owner] += product(offset)

        span = 2 * inner

        @pl.loop(0, span)
        def _(turn, bucket=bucket):
            other = bucket * span + lax.rem(me + turn, span)

            @pl.when(other != me)
            def _():
                out_copy(other).start()

    out_ref[me] = ybuf[me]

    wait_all(out_ref, out_sem)
    pltpu.make_async_copy(whole, whole, part_send).wait()
    wait_all(hbuf, tap_out)
    wait_all(xbuf, sig_out)
    wait_all(ybuf, out_out)


def exchange(signal, filters):
    n, m = lax.axis_size("seq"), lax.axis_size("ch")
    rows, width = signal.shape
    cpd = width // n
    total, pad = n * cpd, 6 * cpd
    blocks = n * rows // LANES + 1
    groups = filters.shape[1] // m
    vmem = pl.BlockSpec(memory_space=pltpu.VMEM)
    return pl.pallas_call(
        functools.partial(exchange_kernel, n, m),
        out_shape=jax.ShapeDtypeStruct((n, cpd, rows), F32),
        in_specs=[vmem, vmem],
        out_specs=vmem,
        scratch_shapes=[
            pltpu.VMEM((n, cpd, rows), F32),
            pltpu.VMEM((m, groups, LANES), F32),
            pltpu.VMEM((m, groups, LANES), F32),
            pltpu.VMEM((groups, 1, rows), F32),
            pltpu.VMEM((n, cpd, rows), F32),
            pltpu.VMEM((n + 1, 1, rows), F32),
            pltpu.VMEM((n, cpd, rows), F32),
            pltpu.VMEM((pad + total, 2 * rows), BF),
            pltpu.VMEM((pad + total, 2 * rows), BF),
            pltpu.VMEM((blocks, LANES, LANES), BF),
            pltpu.VMEM((blocks, LANES, LANES), BF),
            *[pltpu.SemaphoreType.DMA] * 8,
        ],
        compiler_params=pltpu.CompilerParams(
            collective_id=0, has_side_effects=True, vmem_limit_bytes=48 * 1024 * 1024
        ),
    )(signal, filters)


def body(signal, filters, skip_gain):
    rows, width = signal.shape
    values = exchange(signal, filters)
    return values.reshape(width, rows).T + skip_gain[None, :] * signal


def solution(mesh):
    placed = (P("seq", "ch"), P(("seq", "ch"), None), P("ch"))
    return jax.shard_map(
        body, mesh=mesh, in_specs=placed, out_specs=P("seq", "ch"), check_vma=False
    )
```

```python
import functools

import jax
import jax.numpy as jnp
from jax import lax
from jax.experimental import pallas as pl
from jax.experimental.pallas import tpu as pltpu
from jax.sharding import PartitionSpec as P

GROUP = 16
LANES = 128
MESH = pl.DeviceIdType.MESH
BF = jnp.bfloat16
F32 = jnp.float32


def split(value):
    high = value.astype(BF)
    return high, (value - high.astype(F32)).astype(BF)


def swap(left, right):
    half = left.shape[1] // 2
    first = lax.broadcasted_iota(jnp.int32, left.shape, 1) < half
    return (
        jnp.where(first, left, pltpu.roll(right, half, 1)),
        jnp.where(first, pltpu.roll(left, half, 1), right),
    )


def exchange_kernel(
    n, m, sig_in, tap_in, out_ref, sig_ref, part_out, part_in, tap_ref, xbuf, hbuf, ybuf, landed, xx_hi, xx_lo,
    ysum, strip_hi, strip_lo, part_send, tap_out, part_sem, tap_sem, sig_out, out_out, sig_sem, out_sem,
):
    me = lax.axis_index("seq")
    mine = lax.axis_index("ch")
    cpd, rows = sig_ref.shape[2], 2 * LANES
    per = rows // LANES
    barrier = pltpu.get_barrier_semaphore()

    def peer(step):
        away = n // 2 - step // 2
        return lax.rem(me + jnp.where(step % 2 == 1, away, n - away), n)

    @pl.loop(1, n)
    def _(step):
        pl.semaphore_signal(barrier, inc=1, device_id={"seq": peer(step)}, device_id_type=MESH)

    @pl.loop(1, m)
    def _(step):
        pl.semaphore_signal(barrier, inc=1, device_id={"ch": lax.rem(mine + step, m)}, device_id_type=MESH)

    lags = tap_in.shape[0]
    slots = LANES // lags
    tiled = jnp.concatenate([tap_in[...]] * slots, axis=0).T
    lane = lax.broadcasted_iota(jnp.int32, tiled.shape, 1)
    start = lags * lax.rem(mine, slots)
    tiled = jnp.where((lane >= start) & (lane < start + lags), tiled, 0.0)
    part_out[...] = tiled.reshape(part_out.shape)

    for first in range(0, n * cpd, LANES):
        turned = sig_in[:, first:first + LANES].T
        turned = turned.reshape(LANES // cpd, cpd, rows)
        for half, value in enumerate(swap(turned[:, :, :LANES], turned[:, :, LANES:])):
            sig_ref[half, first // cpd:(first + LANES) // cpd] = value

    pl.semaphore_wait(barrier, n + m - 2)

    def part_copy(step):
        other = lax.rem(mine + step, m)
        return pltpu.make_async_remote_copy(
            src_ref=part_out.at[other], dst_ref=part_in.at[mine], send_sem=part_send,
            recv_sem=part_sem, device_id={"ch": other}, device_id_type=MESH,
        )

    def tap_copy(step):
        other = peer(step)
        return pltpu.make_async_remote_copy(
            src_ref=tap_ref.at[other // 2], dst_ref=hbuf.at[me + 1], send_sem=tap_out,
            recv_sem=tap_sem, device_id={"seq": other}, device_id_type=MESH,
        )

    def sig_copy(step, half):
        other = peer(step)
        return pltpu.make_async_remote_copy(
            src_ref=sig_ref.at[half, other], dst_ref=xbuf.at[half, me], send_sem=sig_out.at[half],
            recv_sem=sig_sem.at[half], device_id={"seq": other}, device_id_type=MESH,
        )

    def out_copy(other, half):
        return pltpu.make_async_remote_copy(
            src_ref=ybuf.at[half, other], dst_ref=landed.at[half, me], send_sem=out_out.at[half],
            recv_sem=out_sem.at[half], device_id={"seq": other}, device_id_type=MESH,
        )

    @pl.loop(1, m)
    def _(step):
        part_copy(step).start()

    ahead = n // 4

    @pl.loop(1, ahead)
    def _(step):
        sig_copy(step, 0).start()

    part_in[mine] = part_out[mine]
    whole = part_in.at[pl.ds(0, m - 1)]
    pltpu.make_async_copy(whole, whole, part_sem).wait()
    for half in range(m // slots):
        value = part_in[half * slots]
        for slot in range(1, slots):
            value = value + part_in[half * slots + slot]
        for group in range(n // 2):
            tap_ref[group, :, half * LANES:(half + 1) * LANES] = value[group:group + 1]

    @pl.loop(ahead, ahead + 4)
    def _(step):
        sig_copy(step, 0).start()

    @pl.loop(1, n)
    def _(step):
        tap_copy(step).start()

    @pl.loop(ahead + 4, n)
    def _(step):
        sig_copy(step, 0).start()

    @pl.loop(1, n)
    def _(step):
        sig_copy(step, 1).start()

    hbuf[0] = jnp.zeros((1, rows), F32)
    hbuf[me + 1] = tap_ref[me // 2]
    for half in range(2):
        xbuf[half, me] = sig_ref[half, me]

    def wait_all(ref, sem):
        whole = ref.at[pl.ds(0, n - 1)]
        pltpu.make_async_copy(whole, whole, sem).wait()

    wait_all(hbuf, tap_sem)

    strip_hi[0] = jnp.zeros((LANES, LANES), BF)
    strip_lo[0] = jnp.zeros((LANES, LANES), BF)

    def build(pair, block):
        spread = jnp.broadcast_to(pair, (LANES, 2 * LANES))
        rolled = pltpu.roll(spread, 0, 1, stride=1, stride_axis=0)[:, LANES:]
        high, low = split(rolled)
        strip_hi[block] = high
        strip_lo[block] = low

    @pl.loop(0, n)
    def _(source):
        before = hbuf[source, :, rows - LANES:]
        build(jnp.concatenate([before, hbuf[source + 1, :, :LANES]], axis=1), source * per + 1)
        for part in range(1, per):
            pair = hbuf[source + 1, :, (part - 1) * LANES:(part + 1) * LANES]
            build(pair, source * per + part + 1)

    deep = cpd // 2
    total = n * deep
    depth = xx_hi.shape[1] // rows

    def toeplitz(strip, step):
        first = step * depth * per

        def line(start):
            return jnp.concatenate([strip[start + part] for part in range(per)], axis=1)

        lines = []
        for lag in range(depth):
            for part in range(per):
                lines.append(line(first + lag * per + 1 - part))
        return jnp.concatenate(lines, axis=0)

    @pl.loop(0, 2)
    def _(half):
        wait_all(xbuf.at[half], sig_sem.at[half])

        pairs = xbuf[half].reshape(n // 2, 2 * cpd, LANES)
        sides = swap(pairs[:, :cpd], pairs[:, cpd:])
        value = jnp.concatenate([side.reshape(total, LANES) for side in sides], axis=1)
        row = lax.broadcasted_iota(jnp.int32, value.shape, 0)
        for lag in range(depth):
            shifted = value
            if lag > 0:
                shifted = jnp.where(row < lag * deep, 0.0, pltpu.roll(value, lag * deep, 0))
            high, low = split(shifted)
            xx_hi[:, lag * rows:(lag + 1) * rows] = high
            xx_lo[:, lag * rows:(lag + 1) * rows] = low

        for step in range(n // depth):
            base = step * depth * deep
            height = total - base
            weight_hi, weight_lo = toeplitz(strip_hi, step), toeplitz(strip_lo, step)
            lhs_hi, lhs_lo = xx_hi[:height], xx_lo[:height]
            dot = functools.partial(jnp.dot, preferred_element_type=F32)
            value = dot(lhs_hi, weight_hi) + dot(lhs_lo, weight_hi) + dot(lhs_hi, weight_lo)
            if step > 0:
                value = value + ysum[base:]
            ysum[base:] = value
            done = value[:depth * deep].reshape(depth // 2, cpd, rows)
            for odd, side in enumerate(swap(done[:, :, :LANES], done[:, :, LANES:])):
                for pair in range(depth // 2):
                    ybuf[half, step * depth + 2 * pair + odd] = side[pair]

            @pl.loop(step * depth, (step + 1) * depth)
            def _(other):
                @pl.when(other != me)
                def _():
                    out_copy(other, half).start()

    for half in range(2):
        landed[half, me] = ybuf[half, me]
        wait_all(landed.at[half], out_sem.at[half])
    for side, value in enumerate(swap(landed[0], landed[1])):
        out_ref[:, :, side * LANES:(side + 1) * LANES] = value

    pltpu.make_async_copy(whole, whole, part_send).wait()
    wait_all(hbuf, tap_out)
    for half in range(2):
        wait_all(xbuf.at[half], sig_out.at[half])
        wait_all(ybuf.at[half], out_out.at[half])


def exchange(signal, filters):
    n, m = lax.axis_size("seq"), lax.axis_size("ch")
    rows, width = signal.shape
    cpd = width // n
    total, depth = n * cpd // 2, 4
    message = (2, n, cpd, LANES)
    blocks = n * rows // LANES + 1
    groups = filters.shape[1] // m
    vmem = pl.BlockSpec(memory_space=pltpu.VMEM)
    return pl.pallas_call(
        functools.partial(exchange_kernel, n, m),
        out_shape=jax.ShapeDtypeStruct((n, cpd, rows), F32),
        in_specs=[vmem, vmem],
        out_specs=vmem,
        scratch_shapes=[
            pltpu.VMEM(message, F32),
            pltpu.VMEM((m, groups, LANES), F32),
            pltpu.VMEM((m, groups, LANES), F32),
            pltpu.VMEM((groups, 1, rows), F32),
            pltpu.VMEM(message, F32),
            pltpu.VMEM((n + 1, 1, rows), F32),
            pltpu.VMEM(message, F32),
            pltpu.VMEM(message, F32),
            pltpu.VMEM((total, depth * rows), BF),
            pltpu.VMEM((total, depth * rows), BF),
            pltpu.VMEM((total, rows), F32),
            pltpu.VMEM((blocks, LANES, LANES), BF),
            pltpu.VMEM((blocks, LANES, LANES), BF),
            *[pltpu.SemaphoreType.DMA] * 4,
            *[pltpu.SemaphoreType.DMA((2,))] * 4,
        ],
        compiler_params=pltpu.CompilerParams(
            collective_id=0, has_side_effects=True, vmem_limit_bytes=48 * 1024 * 1024
        ),
    )(signal, filters)


def body(signal, filters, skip_gain):
    rows, width = signal.shape
    values = exchange(signal, filters)
    return values.reshape(width, rows).T + skip_gain[None, :] * signal


def solution(mesh):
    placed = (P("seq", "ch"), P(("seq", "ch"), None), P("ch"))
    return jax.shard_map(
        body, mesh=mesh, in_specs=placed, out_specs=P("seq", "ch"), check_vma=False
    )
```

```python
import functools

import jax
import jax.numpy as jnp
from jax import lax
from jax.experimental import pallas as pl
from jax.experimental.pallas import tpu as pltpu
from jax.sharding import PartitionSpec as P

GROUP = 16
LANES = 128
MESH = pl.DeviceIdType.MESH
BF = jnp.bfloat16
F32 = jnp.float32


def split(value):
    high = value.astype(BF)
    return high, (value - high.astype(F32)).astype(BF)


def swap(left, right):
    half = left.shape[1] // 2
    first = lax.broadcasted_iota(jnp.int32, left.shape, 1) < half
    return (
        jnp.where(first, left, pltpu.roll(right, half, 1)),
        jnp.where(first, pltpu.roll(left, half, 1), right),
    )


def exchange_kernel(
    n, m, sig_in, tap_in, out_ref, sig_ref, part_out, part_in, tap_ref, xbuf, hbuf, ybuf, landed, xx_hi, xx_lo,
    ysum, strip_hi, strip_lo, part_send, tap_out, part_sem, tap_sem, sig_out, out_out, sig_sem, out_sem,
):
    me = lax.axis_index("seq")
    mine = lax.axis_index("ch")
    cpd, rows = sig_ref.shape[2], 2 * LANES
    per = rows // LANES
    barrier = pltpu.get_barrier_semaphore()

    def peer(step):
        away = n // 2 - step // 2
        return lax.rem(me + jnp.where(step % 2 == 1, away, n - away), n)

    @pl.loop(1, n)
    def _(step):
        pl.semaphore_signal(barrier, inc=1, device_id={"seq": peer(step)}, device_id_type=MESH)

    @pl.loop(1, m)
    def _(step):
        pl.semaphore_signal(barrier, inc=1, device_id={"ch": lax.rem(mine + step, m)}, device_id_type=MESH)

    lags = tap_in.shape[0]
    slots = LANES // lags
    tiled = jnp.concatenate([tap_in[...]] * slots, axis=0).T
    lane = lax.broadcasted_iota(jnp.int32, tiled.shape, 1)
    start = lags * lax.rem(mine, slots)
    tiled = jnp.where((lane >= start) & (lane < start + lags), tiled, 0.0)
    part_out[...] = tiled.reshape(part_out.shape)

    for first in range(0, n * cpd, LANES):
        turned = sig_in[:, first:first + LANES].T
        turned = turned.reshape(LANES // cpd, cpd, rows)
        for half, value in enumerate(swap(turned[:, :, :LANES], turned[:, :, LANES:])):
            sig_ref[half, first // cpd:(first + LANES) // cpd] = value

    pl.semaphore_wait(barrier, n + m - 2)

    def part_copy(step):
        other = lax.rem(mine + step, m)
        return pltpu.make_async_remote_copy(
            src_ref=part_out.at[other], dst_ref=part_in.at[mine], send_sem=part_send,
            recv_sem=part_sem, device_id={"ch": other}, device_id_type=MESH,
        )

    def tap_copy(step):
        other = peer(step)
        return pltpu.make_async_remote_copy(
            src_ref=tap_ref.at[other // 2], dst_ref=hbuf.at[me + 1], send_sem=tap_out,
            recv_sem=tap_sem, device_id={"seq": other}, device_id_type=MESH,
        )

    def sig_copy(step, half):
        other = peer(step)
        return pltpu.make_async_remote_copy(
            src_ref=sig_ref.at[half, other], dst_ref=xbuf.at[half, me], send_sem=sig_out.at[half],
            recv_sem=sig_sem.at[half], device_id={"seq": other}, device_id_type=MESH,
        )

    def out_copy(other, half):
        return pltpu.make_async_remote_copy(
            src_ref=ybuf.at[half, other], dst_ref=landed.at[half, me], send_sem=out_out.at[half],
            recv_sem=out_sem.at[half], device_id={"seq": other}, device_id_type=MESH,
        )

    @pl.loop(1, m)
    def _(step):
        part_copy(step).start()

    ahead = n // 4

    @pl.loop(1, ahead)
    def _(step):
        sig_copy(step, 0).start()

    part_in[mine] = part_out[mine]
    whole = part_in.at[pl.ds(0, m - 1)]
    pltpu.make_async_copy(whole, whole, part_sem).wait()
    for half in range(m // slots):
        value = part_in[half * slots]
        for slot in range(1, slots):
            value = value + part_in[half * slots + slot]
        for group in range(n // 2):
            tap_ref[group, :, half * LANES:(half + 1) * LANES] = value[group:group + 1]

    @pl.loop(ahead, ahead + 4)
    def _(step):
        sig_copy(step, 0).start()

    @pl.loop(1, n)
    def _(step):
        tap_copy(step).start()

    @pl.loop(ahead + 4, n)
    def _(step):
        sig_copy(step, 0).start()

    @pl.loop(1, n)
    def _(step):
        sig_copy(step, 1).start()

    hbuf[0] = jnp.zeros((1, rows), F32)
    hbuf[me + 1] = tap_ref[me // 2]
    for half in range(2):
        xbuf[half, me] = sig_ref[half, me]

    def wait_all(ref, sem):
        whole = ref.at[pl.ds(0, n - 1)]
        pltpu.make_async_copy(whole, whole, sem).wait()

    wait_all(hbuf, tap_sem)

    strip_hi[0] = jnp.zeros((LANES, LANES), BF)
    strip_lo[0] = jnp.zeros((LANES, LANES), BF)

    def build(pair, block):
        spread = jnp.broadcast_to(pair, (LANES, 2 * LANES))
        rolled = pltpu.roll(spread, 0, 1, stride=1, stride_axis=0)[:, LANES:]
        high, low = split(rolled)
        strip_hi[block] = high
        strip_lo[block] = low

    @pl.loop(0, n)
    def _(source):
        before = hbuf[source, :, rows - LANES:]
        build(jnp.concatenate([before, hbuf[source + 1, :, :LANES]], axis=1), source * per + 1)
        for part in range(1, per):
            pair = hbuf[source + 1, :, (part - 1) * LANES:(part + 1) * LANES]
            build(pair, source * per + part + 1)

    deep = cpd // 2
    total = n * deep
    depth = xx_hi.shape[1] // rows

    def toeplitz(strip, step):
        first = step * depth * per

        def line(start):
            return jnp.concatenate([strip[start + part] for part in range(per)], axis=1)

        lines = []
        for lag in range(depth):
            for part in range(per):
                lines.append(line(first + lag * per + 1 - part))
        return jnp.concatenate(lines, axis=0)

    @pl.loop(0, 2)
    def _(half):
        wait_all(xbuf.at[half], sig_sem.at[half])

        pairs = xbuf[half].reshape(n // 2, 2 * cpd, LANES)
        sides = swap(pairs[:, :cpd], pairs[:, cpd:])
        value = jnp.concatenate([side.reshape(total, LANES) for side in sides], axis=1)
        row = lax.broadcasted_iota(jnp.int32, value.shape, 0)
        for lag in range(depth):
            shifted = value
            if lag > 0:
                shifted = jnp.where(row < lag * deep, 0.0, pltpu.roll(value, lag * deep, 0))
            high, low = split(shifted)
            xx_hi[:, lag * rows:(lag + 1) * rows] = high
            xx_lo[:, lag * rows:(lag + 1) * rows] = low

        for step in range(n // depth):
            base = step * depth * deep
            height = total - base
            weight_hi, weight_lo = toeplitz(strip_hi, step), toeplitz(strip_lo, step)
            lhs_hi, lhs_lo = xx_hi[:height], xx_lo[:height]
            dot = functools.partial(jnp.dot, preferred_element_type=F32)
            value = dot(lhs_hi, weight_hi) + dot(lhs_lo, weight_hi) + dot(lhs_hi, weight_lo)
            if step > 0:
                value = value + ysum[base:]
            ysum[base:] = value
            done = value[:depth * deep].reshape(depth // 2, cpd, rows)
            for odd, side in enumerate(swap(done[:, :, :LANES], done[:, :, LANES:])):
                for pair in range(depth // 2):
                    ybuf[half, step * depth + 2 * pair + odd] = side[pair]

            @pl.loop(step * depth, (step + 1) * depth)
            def _(other):
                @pl.when(other != me)
                def _():
                    out_copy(other, half).start()

    for half in range(2):
        landed[half, me] = ybuf[half, me]
        wait_all(landed.at[half], out_sem.at[half])
    for first in range(0, n * cpd, LANES):
        peers = slice(first // cpd, (first + LANES) // cpd)
        sides = swap(landed[0, peers], landed[1, peers])
        value = jnp.concatenate([side.reshape(LANES, LANES).T for side in sides], axis=0)
        out_ref[:, first:first + LANES] = value

    pltpu.make_async_copy(whole, whole, part_send).wait()
    wait_all(hbuf, tap_out)
    for half in range(2):
        wait_all(xbuf.at[half], sig_out.at[half])
        wait_all(ybuf.at[half], out_out.at[half])


def exchange(signal, filters):
    n, m = lax.axis_size("seq"), lax.axis_size("ch")
    rows, width = signal.shape
    cpd = width // n
    total, depth = n * cpd // 2, 4
    message = (2, n, cpd, LANES)
    blocks = n * rows // LANES + 1
    groups = filters.shape[1] // m
    vmem = pl.BlockSpec(memory_space=pltpu.VMEM)
    return pl.pallas_call(
        functools.partial(exchange_kernel, n, m),
        out_shape=jax.ShapeDtypeStruct(signal.shape, F32),
        in_specs=[vmem, vmem],
        out_specs=vmem,
        scratch_shapes=[
            pltpu.VMEM(message, F32),
            pltpu.VMEM((m, groups, LANES), F32),
            pltpu.VMEM((m, groups, LANES), F32),
            pltpu.VMEM((groups, 1, rows), F32),
            pltpu.VMEM(message, F32),
            pltpu.VMEM((n + 1, 1, rows), F32),
            pltpu.VMEM(message, F32),
            pltpu.VMEM(message, F32),
            pltpu.VMEM((total, depth * rows), BF),
            pltpu.VMEM((total, depth * rows), BF),
            pltpu.VMEM((total, rows), F32),
            pltpu.VMEM((blocks, LANES, LANES), BF),
            pltpu.VMEM((blocks, LANES, LANES), BF),
            *[pltpu.SemaphoreType.DMA] * 4,
            *[pltpu.SemaphoreType.DMA((2,))] * 4,
        ],
        compiler_params=pltpu.CompilerParams(
            collective_id=0, has_side_effects=True, vmem_limit_bytes=48 * 1024 * 1024
        ),
    )(signal, filters)


def body(signal, filters, skip_gain):
    return exchange(signal, filters) + skip_gain[None, :] * signal


def solution(mesh):
    placed = (P("seq", "ch"), P(("seq", "ch"), None), P("ch"))
    return jax.shard_map(
        body, mesh=mesh, in_specs=placed, out_specs=P("seq", "ch"), check_vma=False
    )
```

```python
import functools

import jax
import jax.numpy as jnp
from jax import lax
from jax.experimental import pallas as pl
from jax.experimental.pallas import tpu as pltpu
from jax.sharding import PartitionSpec as P

GROUP = 16
LANES = 128
MESH = pl.DeviceIdType.MESH
BF = jnp.bfloat16
F32 = jnp.float32


def split(value):
    high = value.astype(BF)
    return high, (value - high.astype(F32)).astype(BF)


def swap(left, right):
    half = left.shape[1] // 2
    first = lax.broadcasted_iota(jnp.int32, left.shape, 1) < half
    return (
        jnp.where(first, left, pltpu.roll(right, half, 1)),
        jnp.where(first, pltpu.roll(left, half, 1), right),
    )


def exchange_kernel(
    n, m, sig_in, tap_in, out_ref, sig_ref, part_out, part_in, tap_ref, xbuf, hbuf, ybuf, landed, xx_hi, xx_lo,
    ysum, strip_hi, strip_lo, part_send, tap_out, part_sem, tap_sem, sig_out, out_out, sig_sem, out_sem,
):
    me = lax.axis_index("seq")
    mine = lax.axis_index("ch")
    cpd, rows = sig_ref.shape[2], 2 * LANES
    per = rows // LANES
    barrier = pltpu.get_barrier_semaphore()

    def peer(step):
        away = n // 2 - step // 2
        return lax.rem(me + jnp.where(step % 2 == 1, away, n - away), n)

    @pl.loop(1, n)
    def _(step):
        pl.semaphore_signal(barrier, inc=1, device_id={"seq": peer(step)}, device_id_type=MESH)

    @pl.loop(1, m)
    def _(step):
        pl.semaphore_signal(barrier, inc=1, device_id={"ch": lax.rem(mine + step, m)}, device_id_type=MESH)

    lags = tap_in.shape[0]
    slots = LANES // lags
    tiled = jnp.concatenate([tap_in[...]] * slots, axis=0).T
    lane = lax.broadcasted_iota(jnp.int32, tiled.shape, 1)
    start = lags * lax.rem(mine, slots)
    tiled = jnp.where((lane >= start) & (lane < start + lags), tiled, 0.0)
    part_out[...] = tiled.reshape(part_out.shape)

    for first in range(0, n * cpd, LANES):
        turned = sig_in[:, first:first + LANES].T
        turned = turned.reshape(LANES // cpd, cpd, rows)
        for half, value in enumerate(swap(turned[:, :, :LANES], turned[:, :, LANES:])):
            sig_ref[half, first // cpd:(first + LANES) // cpd] = value

    pl.semaphore_wait(barrier, n + m - 2)

    def part_copy(step):
        other = lax.rem(mine + step, m)
        return pltpu.make_async_remote_copy(
            src_ref=part_out.at[other], dst_ref=part_in.at[mine], send_sem=part_send,
            recv_sem=part_sem, device_id={"ch": other}, device_id_type=MESH,
        )

    def tap_copy(step):
        other = peer(step)
        return pltpu.make_async_remote_copy(
            src_ref=tap_ref.at[other // 2], dst_ref=hbuf.at[me + 1], send_sem=tap_out,
            recv_sem=tap_sem, device_id={"seq": other}, device_id_type=MESH,
        )

    def sig_copy(step, half):
        other = peer(step)
        return pltpu.make_async_remote_copy(
            src_ref=sig_ref.at[half, other], dst_ref=xbuf.at[half, me], send_sem=sig_out.at[half],
            recv_sem=sig_sem.at[half], device_id={"seq": other}, device_id_type=MESH,
        )

    def out_copy(other, half):
        return pltpu.make_async_remote_copy(
            src_ref=ybuf.at[half, other], dst_ref=landed.at[half, me], send_sem=out_out.at[half],
            recv_sem=out_sem.at[half], device_id={"seq": other}, device_id_type=MESH,
        )

    @pl.loop(1, m)
    def _(step):
        part_copy(step).start()

    ahead = n // 4

    @pl.loop(1, ahead)
    def _(step):
        sig_copy(step, 0).start()

    part_in[mine] = part_out[mine]
    whole = part_in.at[pl.ds(0, m - 1)]
    pltpu.make_async_copy(whole, whole, part_sem).wait()
    for half in range(m // slots):
        value = part_in[half * slots]
        for slot in range(1, slots):
            value = value + part_in[half * slots + slot]
        for group in range(n // 2):
            tap_ref[group, :, half * LANES:(half + 1) * LANES] = value[group:group + 1]

    @pl.loop(ahead, ahead + 4)
    def _(step):
        sig_copy(step, 0).start()

    @pl.loop(1, n)
    def _(step):
        tap_copy(step).start()

    @pl.loop(ahead + 4, n)
    def _(step):
        sig_copy(step, 0).start()

    @pl.loop(1, n)
    def _(step):
        sig_copy(step, 1).start()

    hbuf[0] = jnp.zeros((1, rows), F32)
    hbuf[me + 1] = tap_ref[me // 2]
    for half in range(2):
        xbuf[half, me] = sig_ref[half, me]

    def wait_all(ref, sem):
        whole = ref.at[pl.ds(0, n - 1)]
        pltpu.make_async_copy(whole, whole, sem).wait()

    wait_all(hbuf, tap_sem)

    strip_hi[0] = jnp.zeros((LANES, LANES), BF)
    strip_lo[0] = jnp.zeros((LANES, LANES), BF)

    def build(pair, block):
        spread = jnp.broadcast_to(pair, (LANES, 2 * LANES))
        rolled = pltpu.roll(spread, 0, 1, stride=1, stride_axis=0)[:, LANES:]
        high, low = split(rolled)
        strip_hi[block] = high
        strip_lo[block] = low

    @pl.loop(0, n)
    def _(source):
        before = hbuf[source, :, rows - LANES:]
        build(jnp.concatenate([before, hbuf[source + 1, :, :LANES]], axis=1), source * per + 1)
        for part in range(1, per):
            pair = hbuf[source + 1, :, (part - 1) * LANES:(part + 1) * LANES]
            build(pair, source * per + part + 1)

    deep = cpd // 2
    total = n * deep
    depth = xx_hi.shape[1] // rows

    def toeplitz(strip, step):
        first = step * depth * per

        def line(start):
            return jnp.concatenate([strip[start + part] for part in range(per)], axis=1)

        lines = []
        for lag in range(depth):
            for part in range(per):
                lines.append(line(first + lag * per + 1 - part))
        return jnp.concatenate(lines, axis=0)

    @pl.loop(0, 2)
    def _(half):
        wait_all(xbuf.at[half], sig_sem.at[half])

        pairs = xbuf[half].reshape(n // 2, 2 * cpd, LANES)
        sides = swap(pairs[:, :cpd], pairs[:, cpd:])
        value = jnp.concatenate([side.reshape(total, LANES) for side in sides], axis=1)
        row = lax.broadcasted_iota(jnp.int32, value.shape, 0)
        for lag in range(depth):
            shifted = value
            if lag > 0:
                shifted = jnp.where(row < lag * deep, 0.0, pltpu.roll(value, lag * deep, 0))
            high, low = split(shifted)
            xx_hi[:, lag * rows:(lag + 1) * rows] = high
            xx_lo[:, lag * rows:(lag + 1) * rows] = low

        for step in range(n // depth):
            base = step * depth * deep
            height = total - base
            weight_hi, weight_lo = toeplitz(strip_hi, step), toeplitz(strip_lo, step)
            lhs_hi, lhs_lo = xx_hi[:height], xx_lo[:height]
            dot = functools.partial(jnp.dot, preferred_element_type=F32)
            value = dot(lhs_hi, weight_hi) + dot(lhs_lo, weight_hi) + dot(lhs_hi, weight_lo)
            if step > 0:
                value = value + ysum[base:]
            ysum[base:] = value
            done = value[:depth * deep].reshape(depth // 2, cpd, rows)
            for odd, side in enumerate(swap(done[:, :, :LANES], done[:, :, LANES:])):
                for pair in range(depth // 2):
                    ybuf[half, step * depth + 2 * pair + odd] = side[pair]

            @pl.loop(step * depth, (step + 1) * depth)
            def _(other):
                @pl.when((other != me) & (half == 0))
                def _():
                    out_copy(other, half).start()

        @pl.when(half == 1)
        def _():
            @pl.loop(1, n)
            def _(step):
                out_copy(peer(step), half).start()

    for half in range(2):
        landed[half, me] = ybuf[half, me]
        wait_all(landed.at[half], out_sem.at[half])
    for first in range(0, n * cpd, LANES):
        peers = slice(first // cpd, (first + LANES) // cpd)
        sides = swap(landed[0, peers], landed[1, peers])
        value = jnp.concatenate([side.reshape(LANES, LANES).T for side in sides], axis=0)
        out_ref[:, first:first + LANES] = value

    pltpu.make_async_copy(whole, whole, part_send).wait()
    wait_all(hbuf, tap_out)
    for half in range(2):
        wait_all(xbuf.at[half], sig_out.at[half])
        wait_all(ybuf.at[half], out_out.at[half])


def exchange(signal, filters):
    n, m = lax.axis_size("seq"), lax.axis_size("ch")
    rows, width = signal.shape
    cpd = width // n
    total, depth = n * cpd // 2, 4
    message = (2, n, cpd, LANES)
    blocks = n * rows // LANES + 1
    groups = filters.shape[1] // m
    vmem = pl.BlockSpec(memory_space=pltpu.VMEM)
    return pl.pallas_call(
        functools.partial(exchange_kernel, n, m),
        out_shape=jax.ShapeDtypeStruct(signal.shape, F32),
        in_specs=[vmem, vmem],
        out_specs=vmem,
        scratch_shapes=[
            pltpu.VMEM(message, F32),
            pltpu.VMEM((m, groups, LANES), F32),
            pltpu.VMEM((m, groups, LANES), F32),
            pltpu.VMEM((groups, 1, rows), F32),
            pltpu.VMEM(message, F32),
            pltpu.VMEM((n + 1, 1, rows), F32),
            pltpu.VMEM(message, F32),
            pltpu.VMEM(message, F32),
            pltpu.VMEM((total, depth * rows), BF),
            pltpu.VMEM((total, depth * rows), BF),
            pltpu.VMEM((total, rows), F32),
            pltpu.VMEM((blocks, LANES, LANES), BF),
            pltpu.VMEM((blocks, LANES, LANES), BF),
            *[pltpu.SemaphoreType.DMA] * 4,
            *[pltpu.SemaphoreType.DMA((2,))] * 4,
        ],
        compiler_params=pltpu.CompilerParams(
            collective_id=0, has_side_effects=True, vmem_limit_bytes=48 * 1024 * 1024
        ),
    )(signal, filters)


def body(signal, filters, skip_gain):
    return exchange(signal, filters) + skip_gain[None, :] * signal


def solution(mesh):
    placed = (P("seq", "ch"), P(("seq", "ch"), None), P("ch"))
    return jax.shard_map(
        body, mesh=mesh, in_specs=placed, out_specs=P("seq", "ch"), check_vma=False
    )
```
